32 devices in a mesh: gx: 4 (over z), gy: 8 (over y, x, core).
Axes of the slice: x: 2, y: 2, z: 4, core: 2. Of those that a mesh axis runs over, the one named last changes fastest.
Arguments:
- activations: bfloat16 [192, 18432], P('gy', 'gx'), may hold values from -100 to 100
- norm_gain: float32 [18432], P('gx'), may hold values from 0.25 to 1.75
- w_query: bfloat16 [18432, 12288], P('gx', 'gy'), may hold values from -0.046875 to 0.046875
- w_keyval: bfloat16 [18432, 512], P('gx'), may hold values from -0.046875 to 0.046875
- w_output: bfloat16 [12288, 18432], P('gy', 'gx'), may hold values from -0.4375 to 0.4375
- cache_keys: bfloat16 [192, 2048, 256], P(('gx', 'gy')), may hold values from -240 to 240
- cache_values: bfloat16 [192, 2048, 256], P(('gx', 'gy')), may hold values from -6 to 6
- lengths: int32 [192], P(('gx', 'gy')), may hold values from 1 to 2047, as said below
Outputs:
- attn_out: bfloat16 [192, 18432], P('gy', 'gx')
- new_entries: bfloat16 [192, 512], P(('gx', 'gy'))
The draws below stay inside these ranges and needn't reach their ends.
Inputs may be any that keep to these rules, and one draw needn't show every extreme that they name: Cache slots 0 to lengths[b] - 1 of sequence b hold data, the new token stands at position lengths[b]; some sequence has 2047.
All inputs are finite; a program needn't handle non-finite values.
Results may differ from the reference program's by a relative error of at most 0.007.
The reference program's roundings to bfloat16 on the way (of `normed`, `queries`, `keyval`, `weights` and `context`) count: a program that leaves them out, or rounds other values in their place, can miss the bound.
Values may be sent and summed in bfloat16 or wider, within the bound.
A program may use at most 128 MiB of HBM per device.

```python
import jax
import jax.numpy as jnp
from jax import lax

D = 18432
HEADS = 48
HD = 256
CTX = 2048
SEQS = 192


def draw_activations(key, part):
    key_a = jax.random.fold_in(key, 11)
    key_b = jax.random.fold_in(key, 12)
    key_c = jax.random.fold_in(key, 13)
    ramp = jnp.exp(jnp.linspace(0.0, jnp.log(3.0), D)).astype(jnp.float32)
    column_scale = ramp * jnp.exp(jax.random.uniform(key_b, (D,), jnp.float32, 0.0, jnp.log(4.0)))
    row_scale = jnp.exp(jax.random.uniform(key_c, (SEQS, 1), jnp.float32, 0.0, jnp.log(8.0)))
    base = jnp.clip(jax.random.normal(key_a, (SEQS, D), jnp.float32), -4.0, 4.0)
    values = base * row_scale * column_scale[None, :] * 0.25
    return jnp.clip(values, -100.0, 100.0).astype(jnp.bfloat16)


def draw_cache_keys(key, part):
    key_a = jax.random.fold_in(key, 21)
    base = jnp.clip(jax.random.normal(key_a, (SEQS, CTX, HD), jnp.float32), -6.0, 6.0)
    return base.astype(jnp.bfloat16)


def draw_lengths(key, part):
    key_a = jax.random.fold_in(key, 31)
    key_b = jax.random.fold_in(key, 32)
    drawn = jax.random.randint(key_a, (SEQS,), 1, CTX, dtype=jnp.int32)
    chosen = jax.random.randint(key_b, (), 0, SEQS, dtype=jnp.int32)
    where_top = jnp.arange(SEQS, dtype=jnp.int32) == chosen
    return jnp.where(where_top, CTX - 1, drawn).astype(jnp.int32)


def shard_levels(rng, shape, pieces, low, largest):
    level, own = 1.0, jax.random.fold_in(rng, 6)
    for axis_at, parts in pieces:
        draws = jnp.exp(jax.random.uniform(jax.random.fold_in(own, axis_at), (parts,), jnp.float32, low / len(pieces), largest / len(pieces)))
        level = level * jnp.repeat(draws, shape[axis_at] // parts).reshape([-1 if axis == axis_at else 1 for axis in range(len(shape))])
    return level


def normal_values(key, shape, scale, most, shards=(), kind=jnp.bfloat16):
    entries = scale * jax.random.normal(key, shape, jnp.float32)
    if shards:
        entries = entries * shard_levels(key, shape, shards, -0.22, 0.18)
    return jnp.clip(entries, -most, most).astype(kind)


def setup_inputs(seed: int = 0) -> dict:
    arg_keys = jax.random.split(jax.random.key(seed), 9)
    return {
        "activations": draw_activations(jax.random.fold_in(arg_keys[8], 71), 0),
        "norm_gain": jnp.clip(1.0 + 0.15 * jax.random.normal(arg_keys[1], (D,), jnp.float32), 0.25, 1.75),
        "w_query": normal_values(arg_keys[2], (D, HEADS * HD), D ** -0.5, 0.046875, ((0, 4), (1, 8))),
        "w_keyval": normal_values(arg_keys[3], (D, 2 * HD), D ** -0.5, 0.046875, ((0, 4),)),
        "w_output": normal_values(arg_keys[4], (HEADS * HD, D), (HEADS * HD // 64) ** -0.5, 0.4375, ((0, 8), (1, 4))),
        "cache_keys": draw_cache_keys(jax.random.fold_in(arg_keys[8], 71), 0),
        "cache_values": normal_values(arg_keys[6], (SEQS, CTX, HD), 1.0, 6.0, ((0, 32),)),
        "lengths": draw_lengths(jax.random.fold_in(arg_keys[8], 71), 0),
    }


def rotate(vectors, angles):
    half = vectors.shape[-1] // 2
    first_half = vectors[..., :half]
    second_half = vectors[..., half:]
    cosine = jnp.cos(angles)
    sine = jnp.sin(angles)
    return jnp.concatenate([first_half * cosine - second_half * sine, first_half * sine + second_half * cosine], axis=-1)

def reference(activations, norm_gain, w_query, w_keyval, w_output, cache_keys, cache_values, lengths):
    values_f = activations.astype(jnp.float32)
    row_mean = lax.optimization_barrier(jnp.sum(values_f, axis=1, keepdims=True)) / D
    row_square = lax.optimization_barrier(jnp.sum(values_f * values_f, axis=1, keepdims=True)) / D
    row_var = row_square - row_mean * row_mean
    normed = ((values_f - row_mean) * lax.rsqrt(row_var + 1e-05) * norm_gain[None, :]).astype(jnp.bfloat16)
    queries = jnp.dot(normed, w_query, preferred_element_type=jnp.float32).astype(jnp.bfloat16)
    keyval = jnp.dot(normed, w_keyval, preferred_element_type=jnp.float32).astype(jnp.bfloat16)
    half = HD // 2
    inverse_freq = 10000.0 ** (-(jnp.arange(half, dtype=jnp.float32) * 2.0 / HD))
    positions = lengths.astype(jnp.float32)
    angles = positions[:, None] * inverse_freq[None, :]
    query_heads = queries.reshape(SEQS, HEADS, HD).astype(jnp.float32)
    q_rot = rotate(query_heads, angles[:, None, :]).astype(jnp.bfloat16)
    k_rot = rotate(keyval[:, :HD].astype(jnp.float32), angles).astype(jnp.bfloat16)
    new_value = keyval[:, HD:]
    new_entries = jnp.concatenate([k_rot, new_value], axis=1)
    score_scale = 1.0 / HD ** 0.5

    def attend(operands):
        head_q, keys_c, values_c, own_key, own_value, length_one = operands
        scores = jnp.dot(head_q, keys_c.T, preferred_element_type=jnp.float32) * score_scale
        valid = jnp.arange(CTX, dtype=jnp.int32)[None, :] < length_one
        scores = jnp.where(valid, scores, -1e+30)
        own_score = jnp.dot(head_q, own_key, preferred_element_type=jnp.float32) * score_scale
        top = jnp.maximum(lax.optimization_barrier(jnp.max(scores, axis=1)), own_score)
        probs = jnp.where(valid, jnp.exp(scores - top[:, None]), 0.0)
        own_prob = jnp.exp(own_score - top)
        total = lax.optimization_barrier(jnp.sum(probs, axis=1)) + own_prob
        weights = (probs / total[:, None]).astype(jnp.bfloat16)
        own_weight = (own_prob / total).astype(jnp.bfloat16)
        mixed = jnp.dot(weights, values_c, preferred_element_type=jnp.float32)
        mixed = mixed + own_weight.astype(jnp.float32)[:, None] * own_value.astype(jnp.float32)[None, :]
        return mixed.astype(jnp.bfloat16)
    context = lax.map(attend, (q_rot, cache_keys, cache_values, k_rot, new_value, lengths))
    context = context.reshape(SEQS, HEADS * HD)
    attn_out = jnp.dot(context, w_output, preferred_element_type=jnp.float32).astype(jnp.bfloat16)
    return (attn_out, new_entries)
```

```python
import functools

import jax
import jax.numpy as jnp
from jax import lax
from jax.experimental import pallas as pl
from jax.experimental.pallas import tpu as pltpu
from jax.sharding import PartitionSpec as P

D = 18432
HD = 256
HALF = HD // 2
SG = 2
NCH = 6
LCH = 9
F32 = jnp.float32
BF16 = jnp.bfloat16
MESH = pl.DeviceIdType.MESH


def emit(a, b, c, d):
    c[...] = a[...]
    d[...] = b[...]


def kernel(Z, G, acts, gain_h, wq_h, wkv_h, wo_h, ck_h, cv_h, lens,
           out_h, new_h,
           out, new, gain_1, gain, wq, wkv, wo, ck, cv, xall, normed, stz, stg, kvs, kvr, kro, vnew,
           qpart, qrecv, qrel, qsum, rot, qs, qr, qf, cf, cp, cr, ctx, ctxp, ob, sb, os, orr,
           lsem, xs, xr, fs, zs, zr, gs, gr, kss, ksr, qzs, qzr, qrr, qas, qar,
           cas, car, czs, czr, cfs, bs, br, ohs, ohr):
    mz = lax.axis_index("gx")
    g = lax.axis_index("gy")
    C = G // 2
    chip = g // 2
    core = g % 2
    sib = g + 1 - 2 * core
    B, DL = acts.shape
    S = ck.shape[0]
    HL = wq.shape[1] // HD
    BR = G * S
    QW = wq.shape[1]
    K = S // SG
    NC = wo.shape[1] // NCH
    CW = DL // LCH
    sends = []

    zp = [lax.rem(mz + d, Z) for d in range(1, Z)]
    gp = [lax.rem(g + d, G) for d in range(1, G)]

    def peer(s):
        r, bit = 0, 1
        while bit < C:
            r = r + lax.rem(lax.div(chip, bit) + lax.div(s, bit), 2) * bit
            bit *= 2
        return r

    cpn = [peer(jnp.int32(d)) for d in range(1, C)]

    local = [pltpu.make_async_copy(a, b, lsem.at[i]) for i, (a, b) in enumerate(
        [(acts, xall.at[g]), (wkv_h, wkv), (wq_h, wq), (ck_h, ck), (cv_h, cv), (wo_h, wo)])]
    gcopy = pltpu.make_async_copy(gain_h, gain_1, lsem.at[6])
    for i in (0, 2, 1, 3, 4, 5):
        local[i].start()
        if i == 0:
            gcopy.start()
    line = Z == 4
    outer = (mz == 0) | (mz == Z - 1)
    low = mz < 2
    near = jnp.where(low, 1, 2)
    other = 3 - near
    edge = jnp.where(low, 0, 3)
    far = 3 - edge

    barrier = pltpu.get_barrier_semaphore()
    for z in zp:
        pl.semaphore_signal(barrier, inc=1, device_id=(z, g), device_id_type=MESH)
    for h in gp:
        pl.semaphore_signal(barrier, inc=1, device_id=(mz, h), device_id_type=MESH)
    def remote(src, dst, ss, rs, dev):
        return pltpu.make_async_remote_copy(
            src_ref=src, dst_ref=dst, send_sem=ss, recv_sem=rs,
            device_id=dev, device_id_type=MESH)

    def push(src, dst, ss, rs, dev):
        c = remote(src, dst, ss, rs, dev)
        c.start()
        sends.append(c)

    def arrived(dst, rs):
        remote(dst, dst, rs, rs, (mz, sib)).wait_recv()

    local[0].wait()

    def stat(i, carry):
        a, b = carry
        x = xall[g, :, pl.ds(pl.multiple_of(i * CW, 128), CW)].astype(F32)
        return (a + jnp.sum(x, axis=1, keepdims=True),
                b + jnp.sum(x * x, axis=1, keepdims=True))

    zero = jnp.zeros((B, 1), F32)
    s1, s2 = lax.fori_loop(0, LCH, stat, (zero, zero))
    lane = lax.broadcasted_iota(jnp.int32, (B, 128), 1)
    stz[mz] = jnp.where(lane == 0, s1, s2)
    pl.semaphore_wait(barrier, Z + G - 2)
    for d, z in enumerate(zp):
        push(stz.at[mz], stz.at[mz], zs.at[d], zr.at[mz], (z, g))

    def give(d):
        push(acts, xall.at[g], xs.at[d], xr.at[g], (mz, 2 * cpn[d - 1] + core))

    early = [d for d in range(1, C) if d & (d - 1) == 0]
    late = [d for d in range(1, C) if d & (d - 1)]
    for d in early:
        give(d)
    push(acts, xall.at[g], xs.at[0], xr.at[g], (mz, sib))

    index = lax.broadcasted_iota(jnp.int32, (1, HALF), 1)
    fine = jnp.ones((1, HALF), F32)
    coarse = jnp.ones((1, HALF), F32)
    for i in range(1, 16):
        fine = jnp.where(lax.rem(index, 16) == i, 10000.0 ** (-2.0 * i / HD), fine)
    for i in range(1, HALF // 16):
        coarse = jnp.where(lax.div(index, 16) == i, 10000.0 ** (-32.0 * i / HD), coarse)
    freq = fine * coarse
    angles = jnp.concatenate([freq * lens[s].astype(F32) for s in range(S)], axis=0)
    rot[0] = jnp.cos(angles)
    rot[1] = jnp.sin(angles)

    for z in zp:
        arrived(stz.at[z], zr.at[z])
    tot = stz[0]
    for z in range(1, Z):
        tot = tot + stz[z]
    stg[g] = tot
    for d, h in enumerate(gp):
        push(stg.at[g], stg.at[g], gs.at[d], gr.at[g], (mz, h))

    def normalize(c):
        t = jnp.concatenate([stg[2 * c], stg[2 * c + 1]], axis=0)
        mean = t[:, 0:1] / D
        var = t[:, 1:2] / D - mean * mean
        inv = lax.rsqrt(var + 1e-05)
        rows = pl.ds(pl.multiple_of(c * (2 * B), 16), 2 * B)

        def part(i, _):
            cols = pl.ds(pl.multiple_of(i * CW, 128), CW)
            x = jnp.concatenate([xall[2 * c, :, cols].astype(F32),
                                 xall[2 * c + 1, :, cols].astype(F32)], axis=0)
            normed[rows, cols] = ((x - mean) * inv * gain[:, cols]).astype(BF16)
            return 0

        lax.fori_loop(0, LCH, part, 0)

    def forward(s):
        b = 2 * peer(s) + core
        arrived(xall.at[b], xr.at[b])
        remote(xall.at[b], xall.at[b], fs.at[s], xr.at[b], (mz, sib)).start()

    def send_part(t, j):
        direct = jnp.logical_not((t == far) if line else (t == mz))

        @pl.when((t != mz) & direct)
        def _():
            remote(qpart.at[t, j], qrecv.at[j, mz], qzs.at[j, t], qzr.at[j, mz], (t, g)).start()

        if line:
            @pl.when((t == far) & outer)
            def _():
                remote(qpart.at[t, j], qrel.at[j], qzs.at[j, t], qrr.at[j], (near, g)).start()

    def relay(j):
        @pl.when(jnp.logical_not(outer))
        def _():
            arrived(qrel.at[j], qrr.at[j])
            qsum[j] = qpart[far, j] + qrel[j]
            remote(qsum.at[j], qrecv.at[j, mz], qzs.at[j, far], qzr.at[j, mz], (far, g)).start()

    own_step = 0
    bit = 1
    while bit < C:
        own_step = own_step + lax.rem(lax.div(chip, bit) + lax.div(mz, bit), 2) * bit
        bit *= 2

    def step(i):
        if line and C == Z:
            b0 = Z - 1 - mz
            b1 = b0 + 1 - 2 * lax.rem(b0, 2)
            b2 = mz + 1 - 2 * lax.rem(mz, 2)
            swap = b0 + chip == C - 1
            t0 = jnp.where(swap, b1, b0)
            t1 = jnp.where(swap, b0, b1)
            t = jnp.where(i == 0, t0, jnp.where(i == 1, t1, jnp.where(i == 2, b2, mz)))
            return peer(t)
        return jnp.where(i == C - 1, own_step, jnp.where(i < own_step, i, i + 1))

    gcopy.wait()
    gain[...] = gain_1[...].reshape(1, DL)
    arrived(xall.at[sib], xr.at[sib])
    arrived(stg.at[sib], gr.at[sib])

    @pl.when(step(0) > 0)
    def _():
        forward(step(0))

    for d in late:
        give(d)
    local[2].wait()

    def stage(i, _):
        s = step(i)
        t = peer(s)

        @pl.when(s > 0)
        def _():
            b = 2 * t + 1 - core
            arrived(xall.at[b], xr.at[b])
            arrived(stg.at[2 * t], gr.at[2 * t])
            arrived(stg.at[2 * t + 1], gr.at[2 * t + 1])

        normalize(t)
        rows = pl.ds(pl.multiple_of(t * (2 * B), 16), 2 * B)
        for j in range(HL):
            qpart[t, j] = jnp.dot(normed[rows, :], wq[:, j * HD:(j + 1) * HD],
                                  preferred_element_type=F32)
            send_part(t, j)
            if line:
                @pl.when(i == C - 2)
                def _():
                    relay(j)
            if j == HL // 2:
                @pl.when((i < C - 1) & (step(i + 1) > 0))
                def _():
                    forward(step(i + 1))
        return 0

    lax.fori_loop(0, C, stage, 0)
    local[1].wait()
    part = jnp.dot(normed[...], wkv[...], preferred_element_type=F32)
    for z in range(Z):
        for h in range(G):
            r = z * BR + h * S
            kvs[z, h] = part[r:r + S]
    for d, z in enumerate(zp):
        push(kvs.at[z, g], kvr.at[mz], kss.at[d], ksr.at[mz], (z, g))

    co = rot[0]
    si = rot[1]

    def finish(j, _):
        if line:
            first = jnp.where(outer, near, edge)
            for z in (other, first):
                arrived(qrecv.at[j, z], qzr.at[j, z])

            @pl.when(jnp.logical_not(outer))
            def _():
                arrived(qrecv.at[j, far], qzr.at[j, far])
                qpart[mz, j] = qpart[mz, j] + qrecv[j, far]

            q = qpart[mz, j] + (qrecv[j, first] + qrecv[j, other])
        else:
            q = qpart[mz, j]
            for z in zp:
                arrived(qrecv.at[j, z], qzr.at[j, z])
                q = q + qrecv[j, z]
        for h in range(G):
            qs[j, h] = q[h * S:(h + 1) * S].astype(BF16)
        for d, h in enumerate(gp):
            remote(qs.at[j, h], qr.at[j, g], qas.at[j, d], qar.at[j, g], (mz, h)).start()
        qr[j, g] = qs[j, g]
        return 0

    lax.fori_loop(0, HL, finish, 0)
    for z in zp:
        arrived(kvr.at[z], ksr.at[z])
    kv = kvs[mz, g]
    for z in zp:
        kv = kv + kvr[z]
    kv = kv.astype(BF16)
    kf = kv.astype(F32)
    ka, kb = kf[:, :HALF], kf[:, HALF:HD]
    krot = jnp.concatenate([ka * co - kb * si, ka * si + kb * co], axis=1).astype(BF16)
    new[:, :HD] = krot
    new[:, HD:] = kv[:, HD:]
    kro[...] = krot.astype(F32)
    vnew[...] = kf[:, HD:]

    for j in range(HL):
        for h in gp:
            arrived(qr.at[j, h], qar.at[j, h])
        blocks = [qr[j, h].astype(F32) for h in range(G)]
        for s in range(S):
            rows = jnp.concatenate([b[s:s + 1] for b in blocks], axis=0)
            cs, sn = co[s:s + 1], si[s:s + 1]
            a = rows[:, :HALF]
            b = rows[:, HALF:]
            qf[s, j * G:(j + 1) * G, :] = jnp.concatenate(
                [a * cs - b * sn, a * sn + b * cs], axis=1)

    local[3].wait()
    local[4].wait()
    scale = 1.0 / HD**0.5

    def scores(s):
        qb = qf[s].astype(BF16)
        sc = lax.dot_general(qb, ck[s], (((1,), (1,)), ((), ())),
                             preferred_element_type=F32) * scale
        return qb, sc

    def weigh(s, qb, sc):
        valid = lax.broadcasted_iota(jnp.int32, sc.shape, 1) < lens[s]
        sc = jnp.where(valid, sc, -1e30)
        own = jnp.sum(qb.astype(F32) * kro[s:s + 1, :], axis=1, keepdims=True) * scale
        top = jnp.maximum(jnp.max(sc, axis=1, keepdims=True), own)
        p = jnp.where(valid, jnp.exp(sc - top), 0.0)
        po = jnp.exp(own - top)
        inv = 1.0 / (jnp.sum(p, axis=1, keepdims=True) + po)
        return (p * inv).astype(BF16), (po * inv).astype(BF16).astype(F32)

    def attend(group):
        first = [scores(s) for s in group]
        second = [weigh(s, *f) for s, f in zip(group, first)]
        for s, (w, wn) in zip(group, second):
            mixed = jnp.dot(w, cv[s], preferred_element_type=F32)
            mixed = mixed + wn * vnew[s:s + 1, :]
            cf[s] = mixed.astype(BF16).astype(F32)

    def spread(k):
        for h in gp:
            arrived(cr.at[k, h], car.at[k, h])
        for i in range(HL):
            cols = slice(i * HD, (i + 1) * HD)
            ctx[k, mz, :, cols] = jnp.concatenate(
                [cr[k, h, :, cols].astype(F32) for h in range(G)], axis=0).astype(BF16)
        for d, z in enumerate(zp):
            c = remote(ctx.at[k, mz], ctx.at[k, mz], czs.at[k, d], czr.at[k, mz], (z, g))
            if line:
                pl.when(jnp.logical_not(outer & (z == far)))(c.start)
            else:
                c.start()

    for k in range(K):
        attend(range(k * SG, (k + 1) * SG))
        for h in range(G):
            for i in range(HL):
                rows = jnp.concatenate(
                    [cf[s, i * G + h:i * G + h + 1, :] for s in range(k * SG, (k + 1) * SG)],
                    axis=0)
                cp[k, h, :, i * HD:(i + 1) * HD] = rows.astype(BF16)
        for d, h in enumerate(gp):
            push(cp.at[k, h], cr.at[k, g], cas.at[k, d], car.at[k, g], (mz, h))
        cr[k, g] = cp[k, g]
        if k:
            spread(k - 1)
    spread(K - 1)
    if line:
        for k in range(K):
            @pl.when(jnp.logical_not(outer))
            def _():
                arrived(ctx.at[k, far], czr.at[k, far])
                remote(ctx.at[k, far], ctx.at[k, far], cfs.at[k], czr.at[k, far],
                       (edge, g)).start()
    local[5].wait()
    for k in range(K):
        for z in zp:
            if line:
                @pl.when(outer | (z != far))
                def _():
                    arrived(ctx.at[k, z], czr.at[k, z])
            else:
                arrived(ctx.at[k, z], czr.at[k, z])
    M = Z * BR
    src = lax.broadcasted_iota(jnp.int32, (M, M), 1)
    dst = lax.broadcasted_iota(jnp.int32, (M, M), 0)
    GS = G * SG
    target = ((src // GS) % Z) * BR + ((src % GS) // SG) * S + (src // (Z * GS)) * SG + src % SG
    onehot = jnp.where(dst == target, 1.0, 0.0).astype(BF16)
    ctxp[...] = jnp.dot(onehot, ctx[...].reshape(M, QW), preferred_element_type=F32).astype(BF16)

    def cross(j):
        arrived(sb.at[j], br.at[j])
        for d, c2 in enumerate(cpn):
            os[j, c2] = (ob[j, core, c2] + sb[j, c2]).astype(BF16)
            push(os.at[j, c2], orr.at[j, chip], ohs.at[j, d], ohr.at[j, chip],
                 (mz, 2 * c2 + core))

    for j in range(NCH):
        part = jnp.dot(ctxp[...], wo[:, j * NC:(j + 1) * NC],
                       preferred_element_type=F32)
        for c in range(C):
            for p in range(2):
                r = (2 * c + p) * B
                ob[j, p, c] = part[r:r + B]
        push(ob.at[j, 1 - core], sb.at[j], bs.at[j], br.at[j], (mz, sib))
        if j:
            cross(j - 1)
    cross(NCH - 1)
    for j in range(NCH):
        total = ob[j, core, chip] + sb[j, chip]
        for c2 in cpn:
            arrived(orr.at[j, c2], ohr.at[j, c2])
            total = total + orr[j, c2].astype(F32)
        out[:, j * NC:(j + 1) * NC] = total.astype(BF16)
    emits = [pltpu.make_async_copy(out, out_h, lsem.at[7]),
             pltpu.make_async_copy(new, new_h, lsem.at[8])]
    for c in emits:
        c.start()
    for c in sends:
        c.wait_send()
    for c in emits:
        c.wait()
    for d in range(1, C):
        remote(acts, xall.at[g], fs.at[d], xr.at[g], (mz, sib)).wait_send()
    for j in range(HL):
        for d in range(G - 1):
            remote(qs.at[j, 0], qr.at[j, 0], qas.at[j, d], qar.at[j, 0], (mz, sib)).wait_send()

    def sent(i, _):
        t, j = lax.div(i, HL), lax.rem(i, HL)

        @pl.when(t != mz)
        def _():
            remote(qpart.at[t, j], qrecv.at[j, mz], qzs.at[j, t], qzr.at[j, mz], (mz, sib)).wait_send()

        return 0

    lax.fori_loop(0, Z * HL, sent, 0)
    for k in range(K):
        for d, z in enumerate(zp):
            c = remote(ctx.at[k, mz], ctx.at[k, mz], czs.at[k, d], czs.at[k, d], (mz, sib))
            if line:
                pl.when(jnp.logical_not(outer & (z == far)))(c.wait_send)
            else:
                c.wait_send()
        if line:
            c = remote(ctx.at[k, far], ctx.at[k, far], cfs.at[k], cfs.at[k], (mz, sib))
            pl.when(jnp.logical_not(outer))(c.wait_send)


def body(activations, norm_gain, w_query, w_keyval, w_output, cache_keys, cache_values, lengths):
    Z = lax.axis_size("gx")
    G = lax.axis_size("gy")
    C = G // 2
    B, DL = activations.shape
    S, T, _ = cache_keys.shape
    QW = w_query.shape[1]
    HL = QW // HD
    BR = G * S
    K = S // SG
    NC = w_output.shape[1] // NCH
    V = pltpu.VMEM
    sem = pltpu.SemaphoreType.DMA
    scratch = [
        V((B, w_output.shape[1]), BF16), V((S, 2 * HD), BF16),
        V((DL,), F32), V((1, DL), F32),
        V(w_query.shape, BF16), V(w_keyval.shape, BF16), V(w_output.shape, BF16),
        V(cache_keys.shape, BF16), V(cache_values.shape, BF16),
        V((G, B, DL), BF16), V((G * B, DL), BF16),
        V((Z, B, 128), F32), V((G, B, 128), F32),
        V((Z, G, S, 2 * HD), F32), V((Z, S, 2 * HD), F32), V((S, HD), F32), V((S, HD), F32),
        V((Z, HL, BR, HD), F32), V((HL, Z, BR, HD), F32),
        V((HL, BR, HD), F32), V((HL, BR, HD), F32), V((2, S, HALF), F32),
        V((HL, G, S, HD), BF16), V((HL, G, S, HD), BF16),
        V((S, G * HL, HD), F32), V((S, G * HL, HD), F32),
        V((K, G, SG, QW), BF16), V((K, G, SG, QW), BF16),
        V((K, Z, G * SG, QW), BF16), V((Z * BR, QW), BF16),
        V((NCH, 2, C, B, NC), F32), V((NCH, C, B, NC), F32),
        V((NCH, C, B, NC), BF16), V((NCH, C, B, NC), BF16),
        sem((9,)), sem((C,)), sem((G,)), sem((C,)), sem((Z,)), sem((Z,)), sem((G,)), sem((G,)),
        sem((Z,)), sem((Z,)), sem((HL, Z)), sem((HL, Z)), sem((HL,)), sem((HL, G)), sem((HL, G)),
        sem((K, G)), sem((K, G)), sem((K, Z)), sem((K, Z)), sem((K,)), sem((NCH,)), sem((NCH,)),
        sem((NCH, C)), sem((NCH, C)),
    ]
    anyspec = pl.BlockSpec(memory_space=pl.ANY)
    vspec = pl.BlockSpec(memory_space=pltpu.VMEM)
    shapes = (jax.ShapeDtypeStruct((B, w_output.shape[1]), BF16),
              jax.ShapeDtypeStruct((S, 2 * HD), BF16))
    attn, entries = pl.pallas_call(
        functools.partial(kernel, Z, G),
        out_shape=shapes,
        in_specs=[anyspec, anyspec, anyspec, anyspec, anyspec, anyspec, anyspec,
                  pl.BlockSpec(memory_space=pltpu.SMEM)],
        out_specs=(anyspec, anyspec),
        scratch_shapes=scratch,
        compiler_params=pltpu.CompilerParams(
            collective_id=0, has_side_effects=True, vmem_limit_bytes=63 * 1024 * 1024),
        name="mqa_step",
    )(activations, norm_gain, w_query, w_keyval, w_output, cache_keys, cache_values,
      lengths)
    return pl.pallas_call(
        emit,
        out_shape=shapes,
        in_specs=[vspec, vspec],
        out_specs=(vspec, vspec),
        name="emit",
    )(attn, entries)


def solution(mesh):
    return jax.shard_map(
        body,
        mesh=mesh,
        in_specs=(
            P("gy", "gx"),
            P("gx"),
            P("gx", "gy"),
            P("gx", None),
            P("gy", "gx"),
            P(("gx", "gy"), None, None),
            P(("gx", "gy"), None, None),
            P(("gx", "gy")),
        ),
        out_specs=(P("gy", "gx"), P(("gx", "gy"), None)),
        check_vma=False,
    )
```

```python
import functools

import jax
import jax.numpy as jnp
from jax import lax
from jax.experimental import pallas as pl
from jax.experimental.pallas import tpu as pltpu
from jax.sharding import PartitionSpec as P

D = 18432
HD = 256
HALF = HD // 2
SG = 2
NCH = 3
LCH = 9
F32 = jnp.float32
BF16 = jnp.bfloat16
MESH = pl.DeviceIdType.MESH


def emit(a, b, c, d):
    c[...] = a[...]
    d[...] = b[...]


def kernel(Z, G, acts, gain_h, wq_h, wkv_h, wo_h, ck_h, cv_h, lens,
           out_h, new_h,
           out, new, gain_1, gain, wq, wkv, wo, ck, cv, xall, normed, stz, stg, kvs, kvr, kro, vnew,
           qpart, qrecv, qrel, qsum, rot, qs, qr, qf, cf, cp, cr, ctx, ob, sb, os, orr,
           lsem, xs, xr, fs, zs, zr, gs, gr, kss, ksr, qzs, qzr, qrr, qas, qar,
           cas, car, czs, czr, cfs, bs, br, ohs, ohr):
    mz = lax.axis_index("gx")
    g = lax.axis_index("gy")
    C = G // 2
    chip = g // 2
    core = g % 2
    sib = g + 1 - 2 * core
    B, DL = acts.shape
    S = ck.shape[0]
    HL = wq.shape[1] // HD
    BR = G * S
    QW = wq.shape[1]
    K = S // SG
    NC = wo.shape[1] // NCH
    CW = DL // LCH
    sends = []

    zp = [lax.rem(mz + d, Z) for d in range(1, Z)]
    gp = [lax.rem(g + d, G) for d in range(1, G)]

    def peer(s):
        r, bit = 0, 1
        while bit < C:
            r = r + lax.rem(lax.div(chip, bit) + lax.div(s, bit), 2) * bit
            bit *= 2
        return r

    cpn = [peer(jnp.int32(d)) for d in range(1, C)]

    local = [pltpu.make_async_copy(a, b, lsem.at[i]) for i, (a, b) in enumerate(
        [(acts, xall.at[g]), (wkv_h, wkv), (wq_h, wq), (ck_h, ck), (cv_h, cv), (wo_h, wo)])]
    gcopy = pltpu.make_async_copy(gain_h, gain_1, lsem.at[6])
    for i in (0, 2, 1, 3, 4, 5):
        local[i].start()
        if i == 0:
            gcopy.start()
    line = Z == 4
    outer = (mz == 0) | (mz == Z - 1)
    low = mz < 2
    near = jnp.where(low, 1, 2)
    other = 3 - near
    edge = jnp.where(low, 0, 3)
    far = 3 - edge

    barrier = pltpu.get_barrier_semaphore()
    for z in zp:
        pl.semaphore_signal(barrier, inc=1, device_id=(z, g), device_id_type=MESH)
    for h in gp:
        pl.semaphore_signal(barrier, inc=1, device_id=(mz, h), device_id_type=MESH)
    def remote(src, dst, ss, rs, dev):
        return pltpu.make_async_remote_copy(
            src_ref=src, dst_ref=dst, send_sem=ss, recv_sem=rs,
            device_id=dev, device_id_type=MESH)

    def push(src, dst, ss, rs, dev):
        c = remote(src, dst, ss, rs, dev)
        c.start()
        sends.append(c)

    def arrived(dst, rs):
        remote(dst, dst, rs, rs, (mz, sib)).wait_recv()

    local[0].wait()

    def stat(i, carry):
        a, b = carry
        x = xall[g, :, pl.ds(pl.multiple_of(i * CW, 128), CW)].astype(F32)
        return (a + jnp.sum(x, axis=1, keepdims=True),
                b + jnp.sum(x * x, axis=1, keepdims=True))

    zero = jnp.zeros((B, 1), F32)
    s1, s2 = lax.fori_loop(0, LCH, stat, (zero, zero))
    lane = lax.broadcasted_iota(jnp.int32, (B, 128), 1)
    stz[mz] = jnp.where(lane == 0, s1, s2)
    pl.semaphore_wait(barrier, Z + G - 2)
    for d, z in enumerate(zp):
        push(stz.at[mz], stz.at[mz], zs.at[d], zr.at[mz], (z, g))

    def give(d):
        push(acts, xall.at[g], xs.at[d], xr.at[g], (mz, 2 * cpn[d - 1] + core))

    early = [d for d in range(1, C) if d & (d - 1) == 0]
    late = [d for d in range(1, C) if d & (d - 1)]
    for d in early:
        give(d)
    push(acts, xall.at[g], xs.at[0], xr.at[g], (mz, sib))

    index = lax.broadcasted_iota(jnp.int32, (1, HALF), 1)
    fine = jnp.ones((1, HALF), F32)
    coarse = jnp.ones((1, HALF), F32)
    for i in range(1, 16):
        fine = jnp.where(lax.rem(index, 16) == i, 10000.0 ** (-2.0 * i / HD), fine)
    for i in range(1, HALF // 16):
        coarse = jnp.where(lax.div(index, 16) == i, 10000.0 ** (-32.0 * i / HD), coarse)
    freq = fine * coarse
    angles = jnp.concatenate([freq * lens[s].astype(F32) for s in range(S)], axis=0)
    rot[0] = jnp.cos(angles)
    rot[1] = jnp.sin(angles)

    for z in zp:
        arrived(stz.at[z], zr.at[z])
    tot = stz[0]
    for z in range(1, Z):
        tot = tot + stz[z]
    stg[g] = tot
    for d, h in enumerate(gp):
        push(stg.at[g], stg.at[g], gs.at[d], gr.at[g], (mz, h))

    def normalize(c):
        t = jnp.concatenate([stg[2 * c], stg[2 * c + 1]], axis=0)
        mean = t[:, 0:1] / D
        var = t[:, 1:2] / D - mean * mean
        inv = lax.rsqrt(var + 1e-05)
        rows = pl.ds(pl.multiple_of(c * (2 * B), 16), 2 * B)

        def part(i, _):
            cols = pl.ds(pl.multiple_of(i * CW, 128), CW)
            x = jnp.concatenate([xall[2 * c, :, cols].astype(F32),
                                 xall[2 * c + 1, :, cols].astype(F32)], axis=0)
            normed[rows, cols] = ((x - mean) * inv * gain[:, cols]).astype(BF16)
            return 0

        lax.fori_loop(0, LCH, part, 0)

    def forward(s):
        b = 2 * peer(s) + core
        arrived(xall.at[b], xr.at[b])
        remote(xall.at[b], xall.at[b], fs.at[s], xr.at[b], (mz, sib)).start()

    def send_part(t, j):
        direct = jnp.logical_not((t == far) if line else (t == mz))

        @pl.when((t != mz) & direct)
        def _():
            remote(qpart.at[t, j], qrecv.at[j, mz], qzs.at[j, t], qzr.at[j, mz], (t, g)).start()

        if line:
            @pl.when((t == far) & outer)
            def _():
                remote(qpart.at[t, j], qrel.at[j], qzs.at[j, t], qrr.at[j], (near, g)).start()

    def relay(j):
        @pl.when(jnp.logical_not(outer))
        def _():
            arrived(qrel.at[j], qrr.at[j])
            qsum[j] = qpart[far, j] + qrel[j]
            remote(qsum.at[j], qrecv.at[j, mz], qzs.at[j, far], qzr.at[j, mz], (far, g)).start()

    own_step = 0
    bit = 1
    while bit < C:
        own_step = own_step + lax.rem(lax.div(chip, bit) + lax.div(mz, bit), 2) * bit
        bit *= 2

    def step(i):
        if line and C == Z:
            b0 = Z - 1 - mz
            b1 = b0 + 1 - 2 * lax.rem(b0, 2)
            b2 = mz + 1 - 2 * lax.rem(mz, 2)
            swap = b0 + chip == C - 1
            t0 = jnp.where(swap, b1, b0)
            t1 = jnp.where(swap, b0, b1)
            t = jnp.where(i == 0, t0, jnp.where(i == 1, t1, jnp.where(i == 2, b2, mz)))
            return peer(t)
        return jnp.where(i == C - 1, own_step, jnp.where(i < own_step, i, i + 1))

    gcopy.wait()
    gain[...] = gain_1[...].reshape(1, DL)
    arrived(xall.at[sib], xr.at[sib])
    arrived(stg.at[sib], gr.at[sib])

    for d in late:
        give(d)

    @pl.when(step(0) > 0)
    def _():
        forward(step(0))

    local[2].wait()

    def stage(i, _):
        s = step(i)
        t = peer(s)

        @pl.when(s > 0)
        def _():
            b = 2 * t + 1 - core
            arrived(xall.at[b], xr.at[b])
            arrived(stg.at[2 * t], gr.at[2 * t])
            arrived(stg.at[2 * t + 1], gr.at[2 * t + 1])

        normalize(t)
        rows = pl.ds(pl.multiple_of(t * (2 * B), 16), 2 * B)
        for j in range(HL):
            qpart[t, j] = jnp.dot(normed[rows, :], wq[:, j * HD:(j + 1) * HD],
                                  preferred_element_type=F32)
            send_part(t, j)
            if line:
                @pl.when(i == C - 2)
                def _():
                    relay(j)
            if j == HL // 2:
                @pl.when((i < C - 1) & (step(i + 1) > 0))
                def _():
                    forward(step(i + 1))
        return 0

    lax.fori_loop(0, C, stage, 0)
    local[1].wait()
    part = jnp.dot(normed[...], wkv[...], preferred_element_type=F32)
    for z in range(Z):
        for h in range(G):
            r = z * BR + h * S
            kvs[z, h] = part[r:r + S]
    for d, z in enumerate(zp):
        push(kvs.at[z, g], kvr.at[mz], kss.at[d], ksr.at[mz], (z, g))

    co = rot[0]
    si = rot[1]

    def finish(j, _):
        if line:
            first = jnp.where(outer, near, edge)
            for z in (other, first):
                arrived(qrecv.at[j, z], qzr.at[j, z])

            @pl.when(jnp.logical_not(outer))
            def _():
                arrived(qrecv.at[j, far], qzr.at[j, far])
                qpart[mz, j] = qpart[mz, j] + qrecv[j, far]

            q = qpart[mz, j] + (qrecv[j, first] + qrecv[j, other])
        else:
            q = qpart[mz, j]
            for z in zp:
                arrived(qrecv.at[j, z], qzr.at[j, z])
                q = q + qrecv[j, z]
        for h in range(G):
            qs[j, h] = q[h * S:(h + 1) * S].astype(BF16)
        for d, h in enumerate(gp):
            remote(qs.at[j, h], qr.at[j, g], qas.at[j, d], qar.at[j, g], (mz, h)).start()
        qr[j, g] = qs[j, g]
        return 0

    lax.fori_loop(0, HL, finish, 0)
    for z in zp:
        arrived(kvr.at[z], ksr.at[z])
    kv = kvs[mz, g]
    for z in zp:
        kv = kv + kvr[z]
    kv = kv.astype(BF16)
    kf = kv.astype(F32)
    ka, kb = kf[:, :HALF], kf[:, HALF:HD]
    krot = jnp.concatenate([ka * co - kb * si, ka * si + kb * co], axis=1).astype(BF16)
    new[:, :HD] = krot
    new[:, HD:] = kv[:, HD:]
    kro[...] = krot.astype(F32)
    vnew[...] = kf[:, HD:]

    for j in range(HL):
        for h in gp:
            arrived(qr.at[j, h], qar.at[j, h])
        blocks = [qr[j, h].astype(F32) for h in range(G)]
        for s in range(S):
            rows = jnp.concatenate([b[s:s + 1] for b in blocks], axis=0)
            cs, sn = co[s:s + 1], si[s:s + 1]
            a = rows[:, :HALF]
            b = rows[:, HALF:]
            qf[s, j * G:(j + 1) * G, :] = jnp.concatenate(
                [a * cs - b * sn, a * sn + b * cs], axis=1)

    local[3].wait()
    local[4].wait()
    scale = 1.0 / HD**0.5

    def scores(s):
        qb = qf[s].astype(BF16)
        sc = lax.dot_general(qb, ck[s], (((1,), (1,)), ((), ())),
                             preferred_element_type=F32) * scale
        return qb, sc

    def weigh(s, qb, sc):
        valid = lax.broadcasted_iota(jnp.int32, sc.shape, 1) < lens[s]
        sc = jnp.where(valid, sc, -1e30)
        own = jnp.sum(qb.astype(F32) * kro[s:s + 1, :], axis=1, keepdims=True) * scale
        top = jnp.maximum(jnp.max(sc, axis=1, keepdims=True), own)
        p = jnp.where(valid, jnp.exp(sc - top), 0.0)
        po = jnp.exp(own - top)
        inv = 1.0 / (jnp.sum(p, axis=1, keepdims=True) + po)
        return (p * inv).astype(BF16), (po * inv).astype(BF16).astype(F32)

    def attend(group):
        first = [scores(s) for s in group]
        second = [weigh(s, *f) for s, f in zip(group, first)]
        for s, (w, wn) in zip(group, second):
            mixed = jnp.dot(w, cv[s], preferred_element_type=F32)
            mixed = mixed + wn * vnew[s:s + 1, :]
            cf[s] = mixed.astype(BF16).astype(F32)

    def spread(k):
        for h in gp:
            arrived(cr.at[k, h], car.at[k, h])
        for i in range(HL):
            cols = slice(i * HD, (i + 1) * HD)
            ctx[k, mz, :, cols] = jnp.concatenate(
                [cr[k, h, :, cols].astype(F32) for h in range(G)], axis=0).astype(BF16)
        for d, z in enumerate(zp):
            c = remote(ctx.at[k, mz], ctx.at[k, mz], czs.at[k, d], czr.at[k, mz], (z, g))
            if line:
                pl.when(jnp.logical_not(outer & (z == far)))(c.start)
            else:
                c.start()

    for k in range(K):
        attend(range(k * SG, (k + 1) * SG))
        for h in range(G):
            for i in range(HL):
                rows = jnp.concatenate(
                    [cf[s, i * G + h:i * G + h + 1, :] for s in range(k * SG, (k + 1) * SG)],
                    axis=0)
                cp[k, h, :, i * HD:(i + 1) * HD] = rows.astype(BF16)
        for d, h in enumerate(gp):
            push(cp.at[k, h], cr.at[k, g], cas.at[k, d], car.at[k, g], (mz, h))
        cr[k, g] = cp[k, g]
        if k:
            spread(k - 1)
    spread(K - 1)

    def pass_on(k):
        @pl.when(jnp.logical_not(outer))
        def _():
            arrived(ctx.at[k, far], czr.at[k, far])
            remote(ctx.at[k, far], ctx.at[k, far], cfs.at[k], czr.at[k, far],
                   (edge, g)).start()

    def gathered(k):
        for z in zp:
            if line:
                @pl.when(outer | (z != far))
                def _():
                    arrived(ctx.at[k, z], czr.at[k, z])
            else:
                arrived(ctx.at[k, z], czr.at[k, z])

    M = Z * G * SG
    PR = C * SG

    def cross(k, j):
        arrived(sb.at[k, j], br.at[k, j])
        for d, c2 in enumerate(cpn):
            os[k, j, c2] = (ob[k, j, core, c2] + sb[k, j, c2]).astype(BF16)
            push(os.at[k, j, c2], orr.at[k, j, chip], ohs.at[k, j, d], ohr.at[k, j, chip],
                 (mz, 2 * c2 + core))

    local[5].wait()
    pending = []
    for k in range(K):
        if line:
            pass_on(k)
        gathered(k)
        rows = ctx[k].reshape(M, QW)
        for j in range(NCH):
            part = jnp.dot(rows, wo[:, j * NC:(j + 1) * NC], preferred_element_type=F32)
            for c in range(C):
                for p in range(2):
                    r = (2 * c + p) * PR
                    ob[k, j, p, c] = part[r:r + PR]
            push(ob.at[k, j, 1 - core], sb.at[k, j], bs.at[k, j], br.at[k, j], (mz, sib))
            for item in pending:
                cross(*item)
            pending = [(k, j)]
    for item in pending:
        cross(*item)
    src = lax.broadcasted_iota(jnp.int32, (B, B), 1)
    dst = lax.broadcasted_iota(jnp.int32, (B, B), 0)
    target = ((src % PR) // SG) * S + (src // PR) * SG + src % SG
    onehot = jnp.where(dst == target, 1.0, 0.0).astype(BF16)
    for j in range(NCH):
        groups = []
        for k in range(K):
            total = ob[k, j, core, chip] + sb[k, j, chip]
            for c2 in cpn:
                arrived(orr.at[k, j, c2], ohr.at[k, j, c2])
                total = total + orr[k, j, c2].astype(F32)
            groups.append(total)
        ordered = jnp.concatenate(groups, axis=0).astype(BF16)
        out[:, j * NC:(j + 1) * NC] = jnp.dot(
            onehot, ordered, preferred_element_type=F32).astype(BF16)
    emits = [pltpu.make_async_copy(out, out_h, lsem.at[7]),
             pltpu.make_async_copy(new, new_h, lsem.at[8])]
    for c in emits:
        c.start()
    for c in sends:
        c.wait_send()
    for c in emits:
        c.wait()
    for d in range(1, C):
        remote(acts, xall.at[g], fs.at[d], xr.at[g], (mz, sib)).wait_send()
    for j in range(HL):
        for d in range(G - 1):
            remote(qs.at[j, 0], qr.at[j, 0], qas.at[j, d], qar.at[j, 0], (mz, sib)).wait_send()

    def sent(i, _):
        t, j = lax.div(i, HL), lax.rem(i, HL)

        @pl.when(t != mz)
        def _():
            remote(qpart.at[t, j], qrecv.at[j, mz], qzs.at[j, t], qzr.at[j, mz], (mz, sib)).wait_send()

        return 0

    lax.fori_loop(0, Z * HL, sent, 0)
    for k in range(K):
        for d, z in enumerate(zp):
            c = remote(ctx.at[k, mz], ctx.at[k, mz], czs.at[k, d], czs.at[k, d], (mz, sib))
            if line:
                pl.when(jnp.logical_not(outer & (z == far)))(c.wait_send)
            else:
                c.wait_send()
        if line:
            c = remote(ctx.at[k, far], ctx.at[k, far], cfs.at[k], cfs.at[k], (mz, sib))
            pl.when(jnp.logical_not(outer))(c.wait_send)


def body(activations, norm_gain, w_query, w_keyval, w_output, cache_keys, cache_values, lengths):
    Z = lax.axis_size("gx")
    G = lax.axis_size("gy")
    C = G // 2
    B, DL = activations.shape
    S, T, _ = cache_keys.shape
    QW = w_query.shape[1]
    HL = QW // HD
    BR = G * S
    K = S // SG
    NC = w_output.shape[1] // NCH
    V = pltpu.VMEM
    sem = pltpu.SemaphoreType.DMA
    scratch = [
        V((B, w_output.shape[1]), BF16), V((S, 2 * HD), BF16),
        V((DL,), F32), V((1, DL), F32),
        V(w_query.shape, BF16), V(w_keyval.shape, BF16), V(w_output.shape, BF16),
        V(cache_keys.shape, BF16), V(cache_values.shape, BF16),
        V((G, B, DL), BF16), V((G * B, DL), BF16),
        V((Z, B, 128), F32), V((G, B, 128), F32),
        V((Z, G, S, 2 * HD), F32), V((Z, S, 2 * HD), F32), V((S, HD), F32), V((S, HD), F32),
        V((Z, HL, BR, HD), F32), V((HL, Z, BR, HD), F32),
        V((HL, BR, HD), F32), V((HL, BR, HD), F32), V((2, S, HALF), F32),
        V((HL, G, S, HD), BF16), V((HL, G, S, HD), BF16),
        V((S, G * HL, HD), F32), V((S, G * HL, HD), F32),
        V((K, G, SG, QW), BF16), V((K, G, SG, QW), BF16),
        V((K, Z, G * SG, QW), BF16),
        V((K, NCH, 2, C, C * SG, NC), F32), V((K, NCH, C, C * SG, NC), F32),
        V((K, NCH, C, C * SG, NC), BF16), V((K, NCH, C, C * SG, NC), BF16),
        sem((9,)), sem((C,)), sem((G,)), sem((C,)), sem((Z,)), sem((Z,)), sem((G,)), sem((G,)),
        sem((Z,)), sem((Z,)), sem((HL, Z)), sem((HL, Z)), sem((HL,)), sem((HL, G)), sem((HL, G)),
        sem((K, G)), sem((K, G)), sem((K, Z)), sem((K, Z)), sem((K,)), sem((K, NCH)), sem((K, NCH)),
        sem((K, NCH, C)), sem((K, NCH, C)),
    ]
    anyspec = pl.BlockSpec(memory_space=pl.ANY)
    vspec = pl.BlockSpec(memory_space=pltpu.VMEM)
    shapes = (jax.ShapeDtypeStruct((B, w_output.shape[1]), BF16),
              jax.ShapeDtypeStruct((S, 2 * HD), BF16))
    attn, entries = pl.pallas_call(
        functools.partial(kernel, Z, G),
        out_shape=shapes,
        in_specs=[anyspec, anyspec, anyspec, anyspec, anyspec, anyspec, anyspec,
                  pl.BlockSpec(memory_space=pltpu.SMEM)],
        out_specs=(anyspec, anyspec),
        scratch_shapes=scratch,
        compiler_params=pltpu.CompilerParams(
            collective_id=0, has_side_effects=True, vmem_limit_bytes=63 * 1024 * 1024),
        name="mqa_step",
    )(activations, norm_gain, w_query, w_keyval, w_output, cache_keys, cache_values,
      lengths)
    return pl.pallas_call(
        emit,
        out_shape=shapes,
        in_specs=[vspec, vspec],
        out_specs=(vspec, vspec),
        name="emit",
    )(attn, entries)


def solution(mesh):
    return jax.shard_map(
        body,
        mesh=mesh,
        in_specs=(
            P("gy", "gx"),
            P("gx"),
            P("gx", "gy"),
            P("gx", None),
            P("gy", "gx"),
            P(("gx", "gy"), None, None),
            P(("gx", "gy"), None, None),
            P(("gx", "gy")),
        ),
        out_specs=(P("gy", "gx"), P(("gx", "gy"), None)),
        check_vma=False,
    )
```

```python
import functools

import jax
import jax.numpy as jnp
from jax import lax
from jax.experimental import pallas as pl
from jax.experimental.pallas import tpu as pltpu
from jax.sharding import PartitionSpec as P

D = 18432
HD = 256
HALF = HD // 2
SG = 2
NCH = 3
LCH = 9
F32 = jnp.float32
BF16 = jnp.bfloat16
MESH = pl.DeviceIdType.MESH


def emit(a, b, c, d):
    c[...] = a[...]
    d[...] = b[...]


def kernel(Z, G, acts, gain_h, wq_h, wkv_h, wo_h, ck_h, cv_h, lens_h,
           out_h, new_h,
           out, new, lens, gain_1, gain, wq, wkv, wo, ck, cv, xall, normed, stz, stg, kvs, kvr, kro, vnew,
           qpart, qrecv, qrel, qsum, rot, qs, qr, qf, cf, cp, cr, ctx, ob, sb, os, orr,
           lsem, xs, xr, fs, zs, zr, gs, gr, kss, ksr, qzs, qzr, qrr, qas, qar,
           cas, car, bs, br, ohs, ohr):
    mz = lax.axis_index("gx")
    g = lax.axis_index("gy")
    C = G // 2
    chip = g // 2
    core = g % 2
    sib = g + 1 - 2 * core
    B, DL = acts.shape
    S = ck.shape[0]
    HL = wq.shape[1] // HD
    BR = G * S
    QW = wq.shape[1]
    K = S // SG
    NC = wo.shape[1] // NCH
    CW = DL // LCH
    sends = []

    zp = [lax.rem(mz + d, Z) for d in range(1, Z)]
    gp = [lax.rem(g + d, G) for d in range(1, G)]

    def peer(s):
        r, bit = 0, 1
        while bit < C:
            r = r + lax.rem(lax.div(chip, bit) + lax.div(s, bit), 2) * bit
            bit *= 2
        return r

    cpn = [peer(jnp.int32(d)) for d in range(1, C)]

    barrier = pltpu.get_barrier_semaphore()
    N = Z * G
    me = mz * G + g

    def greet(d, _):
        n = lax.rem(me + d, N)
        pl.semaphore_signal(barrier, inc=1, device_id=(lax.div(n, G), lax.rem(n, G)),
                            device_id_type=MESH)
        return 0

    lax.fori_loop(1, N, greet, 0)

    local = [pltpu.make_async_copy(a, b, lsem.at[i]) for i, (a, b) in enumerate(
        [(acts, xall.at[g]), (wkv_h, wkv), (wq_h, wq), (ck_h, ck), (cv_h, cv), (wo_h, wo)])]
    gcopy = pltpu.make_async_copy(gain_h, gain_1, lsem.at[6])
    lcopy = pltpu.make_async_copy(lens_h, lens, lsem.at[9])
    for i in (0, 2, 1, 3, 4, 5):
        local[i].start()
        if i == 0:
            gcopy.start()
            lcopy.start()
    line = Z == 4
    outer = (mz == 0) | (mz == Z - 1)
    low = mz < 2
    near = jnp.where(low, 1, 2)
    other = 3 - near
    edge = jnp.where(low, 0, 3)
    far = 3 - edge

    def remote(src, dst, ss, rs, dev):
        return pltpu.make_async_remote_copy(
            src_ref=src, dst_ref=dst, send_sem=ss, recv_sem=rs,
            device_id=dev, device_id_type=MESH)

    def push(src, dst, ss, rs, dev):
        c = remote(src, dst, ss, rs, dev)
        c.start()
        sends.append(c)

    def arrived(dst, rs):
        remote(dst, dst, rs, rs, (mz, sib)).wait_recv()

    local[0].wait()

    def stat(i, carry):
        a, b = carry
        x = xall[g, :, pl.ds(pl.multiple_of(i * CW, 128), CW)].astype(F32)
        return (a + jnp.sum(x, axis=1, keepdims=True),
                b + jnp.sum(x * x, axis=1, keepdims=True))

    zero = jnp.zeros((B, 1), F32)
    s1, s2 = lax.fori_loop(0, LCH, stat, (zero, zero))
    lane = lax.broadcasted_iota(jnp.int32, (B, 128), 1)
    stz[mz] = jnp.where(lane == 0, s1, s2)
    pl.semaphore_wait(barrier, N - 1)
    for d, z in enumerate(zp):
        push(stz.at[mz], stz.at[mz], zs.at[d], zr.at[mz], (z, g))

    def give(d):
        push(acts, xall.at[g], xs.at[d], xr.at[g], (mz, 2 * cpn[d - 1] + core))

    early = [d for d in range(1, C) if d & (d - 1) == 0]
    late = [d for d in range(1, C) if d & (d - 1)]
    for d in early:
        give(d)
    push(acts, xall.at[g], xs.at[0], xr.at[g], (mz, sib))

    lcopy.wait()
    index = lax.broadcasted_iota(jnp.int32, (1, HALF), 1)
    fine = jnp.ones((1, HALF), F32)
    coarse = jnp.ones((1, HALF), F32)
    for i in range(1, 16):
        fine = jnp.where(lax.rem(index, 16) == i, 10000.0 ** (-2.0 * i / HD), fine)
    for i in range(1, HALF // 16):
        coarse = jnp.where(lax.div(index, 16) == i, 10000.0 ** (-32.0 * i / HD), coarse)
    freq = fine * coarse
    angles = jnp.concatenate([freq * lens[s].astype(F32) for s in range(S)], axis=0)
    rot[0] = jnp.cos(angles)
    rot[1] = jnp.sin(angles)

    for z in zp:
        arrived(stz.at[z], zr.at[z])
    tot = stz[0]
    for z in range(1, Z):
        tot = tot + stz[z]
    stg[g] = tot
    for d, h in enumerate(gp):
        push(stg.at[g], stg.at[g], gs.at[d], gr.at[g], (mz, h))

    def normalize(c, i):
        t = jnp.concatenate([stg[2 * c], stg[2 * c + 1]], axis=0)
        mean = t[:, 0:1] / D
        var = t[:, 1:2] / D - mean * mean
        inv = lax.rsqrt(var + 1e-05)
        rows = pl.ds(pl.multiple_of(i * (2 * B), 16), 2 * B)

        def part(i, _):
            cols = pl.ds(pl.multiple_of(i * CW, 128), CW)
            x = jnp.concatenate([xall[2 * c, :, cols].astype(F32),
                                 xall[2 * c + 1, :, cols].astype(F32)], axis=0)
            normed[rows, cols] = ((x - mean) * inv * gain[:, cols]).astype(BF16)
            return 0

        lax.fori_loop(0, LCH, part, 0)

    def forward(s):
        b = 2 * peer(s) + core
        arrived(xall.at[b], xr.at[b])
        remote(xall.at[b], xall.at[b], fs.at[s], xr.at[b], (mz, sib)).start()

    def send_part(t, j):
        direct = jnp.logical_not((t == far) if line else (t == mz))

        @pl.when((t != mz) & direct)
        def _():
            remote(qpart.at[t, j], qrecv.at[j, mz], qzs.at[j, t], qzr.at[j, mz], (t, g)).start()

        if line:
            @pl.when((t == far) & outer)
            def _():
                remote(qpart.at[t, j], qrel.at[j], qzs.at[j, t], qrr.at[j], (near, g)).start()

    def relay(j):
        @pl.when(jnp.logical_not(outer))
        def _():
            arrived(qrel.at[j], qrr.at[j])
            qsum[j] = qpart[far, j] + qrel[j]
            remote(qsum.at[j], qrecv.at[j, mz], qzs.at[j, far], qzr.at[j, mz], (far, g)).start()

    own_step = 0
    bit = 1
    while bit < C:
        own_step = own_step + lax.rem(lax.div(chip, bit) + lax.div(mz, bit), 2) * bit
        bit *= 2

    def step(i):
        if line and C == Z:
            b0 = Z - 1 - mz
            b1 = b0 + 1 - 2 * lax.rem(b0, 2)
            b2 = mz + 1 - 2 * lax.rem(mz, 2)
            swap = b0 + chip == C - 1
            t0 = jnp.where(swap, b1, b0)
            t1 = jnp.where(swap, b0, b1)
            t = jnp.where(i == 0, t0, jnp.where(i == 1, t1, jnp.where(i == 2, b2, mz)))
            return peer(t)
        return jnp.where(i == C - 1, own_step, jnp.where(i < own_step, i, i + 1))

    gcopy.wait()
    gain[...] = gain_1[...].reshape(1, DL)
    arrived(xall.at[sib], xr.at[sib])
    arrived(stg.at[sib], gr.at[sib])

    for d in late:
        give(d)

    @pl.when(step(0) > 0)
    def _():
        forward(step(0))

    local[2].wait()

    def ready(i):
        s = step(i)
        t = peer(s)

        @pl.when(s > 0)
        def _():
            b = 2 * t + 1 - core
            arrived(xall.at[b], xr.at[b])
            arrived(stg.at[2 * t], gr.at[2 * t])
            arrived(stg.at[2 * t + 1], gr.at[2 * t + 1])

        normalize(t, i)
        return t

    def ahead(i):
        @pl.when(step(i) > 0)
        def _():
            forward(step(i))

    def stage(i, _):
        t = ready(i)
        rows = pl.ds(pl.multiple_of(i * (2 * B), 16), 2 * B)
        for j in range(HL):
            qpart[t, j] = jnp.dot(normed[rows, :], wq[:, j * HD:(j + 1) * HD],
                                  preferred_element_type=F32)
            send_part(t, j)
            if j == HL // 2:
                ahead(i + 1)
        return 0

    lax.fori_loop(0, C - 2, stage, 0)
    ahead(C - 1)
    t = ready(C - 2)
    ready(C - 1)
    for j in range(HL):
        part = jnp.dot(normed[(C - 2) * 2 * B:, :], wq[:, j * HD:(j + 1) * HD],
                       preferred_element_type=F32)
        qpart[t, j] = part[:2 * B]
        qpart[mz, j] = part[2 * B:]
        send_part(t, j)
        if line:
            relay(j)
    local[1].wait()
    part = jnp.dot(normed[...], wkv[...], preferred_element_type=F32)
    for i in range(C):
        z = peer(step(i))
        for h in range(G):
            r = i * BR + h * S
            kvs[z, h] = part[r:r + S]
    for d, z in enumerate(zp):
        push(kvs.at[z, g], kvr.at[mz], kss.at[d], ksr.at[mz], (z, g))

    co = rot[0]
    si = rot[1]

    def finish(j, _):
        if line:
            first = jnp.where(outer, near, edge)
            for z in (other, first):
                arrived(qrecv.at[j, z], qzr.at[j, z])

            @pl.when(jnp.logical_not(outer))
            def _():
                arrived(qrecv.at[j, far], qzr.at[j, far])
                qpart[mz, j] = qpart[mz, j] + qrecv[j, far]

            q = qpart[mz, j] + (qrecv[j, first] + qrecv[j, other])
        else:
            q = qpart[mz, j]
            for z in zp:
                arrived(qrecv.at[j, z], qzr.at[j, z])
                q = q + qrecv[j, z]
        for h in range(G):
            qs[j, h] = q[h * S:(h + 1) * S].astype(BF16)
        for d, h in enumerate(gp):
            remote(qs.at[j, h], qr.at[j, g], qas.at[j, d], qar.at[j, g], (mz, h)).start()
        qr[j, g] = qs[j, g]
        return 0

    lax.fori_loop(0, HL, finish, 0)
    for z in zp:
        arrived(kvr.at[z], ksr.at[z])
    kv = kvs[mz, g]
    for z in zp:
        kv = kv + kvr[z]
    kv = kv.astype(BF16)
    kf = kv.astype(F32)
    ka, kb = kf[:, :HALF], kf[:, HALF:HD]
    krot = jnp.concatenate([ka * co - kb * si, ka * si + kb * co], axis=1).astype(BF16)
    new[:, :HD] = krot
    new[:, HD:] = kv[:, HD:]
    kro[...] = krot.astype(F32)
    vnew[...] = kf[:, HD:]

    for j in range(HL):
        for h in gp:
            arrived(qr.at[j, h], qar.at[j, h])
        blocks = [qr[j, h].astype(F32) for h in range(G)]
        for s in range(S):
            rows = jnp.concatenate([b[s:s + 1] for b in blocks], axis=0)
            cs, sn = co[s:s + 1], si[s:s + 1]
            a = rows[:, :HALF]
            b = rows[:, HALF:]
            qf[s, j * G:(j + 1) * G, :] = jnp.concatenate(
                [a * cs - b * sn, a * sn + b * cs], axis=1)

    local[3].wait()
    local[4].wait()
    scale = 1.0 / HD**0.5

    def scores(s):
        qb = qf[s].astype(BF16)
        sc = lax.dot_general(qb, ck[s], (((1,), (1,)), ((), ())),
                             preferred_element_type=F32) * scale
        return qb, sc

    def weigh(s, qb, sc):
        valid = lax.broadcasted_iota(jnp.int32, sc.shape, 1) < lens[s]
        sc = jnp.where(valid, sc, -1e30)
        own = jnp.sum(qb.astype(F32) * kro[s:s + 1, :], axis=1, keepdims=True) * scale
        top = jnp.maximum(jnp.max(sc, axis=1, keepdims=True), own)
        p = jnp.where(valid, jnp.exp(sc - top), 0.0)
        po = jnp.exp(own - top)
        inv = 1.0 / (jnp.sum(p, axis=1, keepdims=True) + po)
        return (p * inv).astype(BF16), (po * inv).astype(BF16).astype(F32)

    def attend(group):
        first = [scores(s) for s in group]
        second = [weigh(s, *f) for s, f in zip(group, first)]
        for s, (w, wn) in zip(group, second):
            mixed = jnp.dot(w, cv[s], preferred_element_type=F32)
            mixed = mixed + wn * vnew[s:s + 1, :]
            cf[s] = mixed.astype(BF16).astype(F32)

    def scatter(k):
        def one(d, _):
            n = lax.rem(me + d, N)
            z, h = lax.div(n, G), lax.rem(n, G)
            remote(cp.at[k, h], cr.at[k, mz, g], cas.at[k, z, h], car.at[k, mz, g], (z, h)).start()
            return 0

        lax.fori_loop(1, N, one, 0)
        cr[k, mz, g] = cp[k, g]

    def gathered(k):
        def one(d, _):
            n = lax.rem(me + d, N)
            z, h = lax.div(n, G), lax.rem(n, G)
            arrived(cr.at[k, z, h], car.at[k, z, h])
            return 0

        lax.fori_loop(1, N, one, 0)
        for i in range(HL):
            cols = slice(i * HD, (i + 1) * HD)
            ctx[k, :, cols] = jnp.concatenate(
                [cr[k, z, h, :, cols].astype(F32) for z in range(Z) for h in range(G)],
                axis=0).astype(BF16)

    for k in range(K):
        attend(range(k * SG, (k + 1) * SG))
        for h in range(G):
            for i in range(HL):
                rows = jnp.concatenate(
                    [cf[s, i * G + h:i * G + h + 1, :] for s in range(k * SG, (k + 1) * SG)],
                    axis=0)
                cp[k, h, :, i * HD:(i + 1) * HD] = rows.astype(BF16)
        scatter(k)

    M = Z * G * SG
    PR = C * SG

    def cross(k, j):
        arrived(sb.at[k, j], br.at[k, j])
        for d, c2 in enumerate(cpn):
            os[k, j, c2] = (ob[k, j, core, c2] + sb[k, j, c2]).astype(BF16)
            push(os.at[k, j, c2], orr.at[k, j, chip], ohs.at[k, j, d], ohr.at[k, j, chip],
                 (mz, 2 * c2 + core))

    local[5].wait()
    pending = []
    for k in range(K):
        gathered(k)
        rows = ctx[k]
        for j in range(NCH):
            part = jnp.dot(rows, wo[:, j * NC:(j + 1) * NC], preferred_element_type=F32)
            for c in range(C):
                for p in range(2):
                    r = (2 * c + p) * PR
                    ob[k, j, p, c] = part[r:r + PR]
            push(ob.at[k, j, 1 - core], sb.at[k, j], bs.at[k, j], br.at[k, j], (mz, sib))
            for item in pending:
                cross(*item)
            pending = [(k, j)]
    for item in pending:
        cross(*item)
    src = lax.broadcasted_iota(jnp.int32, (B, B), 1)
    dst = lax.broadcasted_iota(jnp.int32, (B, B), 0)
    target = ((src % PR) // SG) * S + (src // PR) * SG + src % SG
    onehot = jnp.where(dst == target, 1.0, 0.0).astype(BF16)
    for j in range(NCH):
        groups = []
        for k in range(K):
            total = ob[k, j, core, chip] + sb[k, j, chip]
            for c2 in cpn:
                arrived(orr.at[k, j, c2], ohr.at[k, j, c2])
                total = total + orr[k, j, c2].astype(F32)
            groups.append(total)
        ordered = jnp.concatenate(groups, axis=0).astype(BF16)
        out[:, j * NC:(j + 1) * NC] = jnp.dot(
            onehot, ordered, preferred_element_type=F32).astype(BF16)
    emits = [pltpu.make_async_copy(out, out_h, lsem.at[7]),
             pltpu.make_async_copy(new, new_h, lsem.at[8])]
    for c in emits:
        c.start()
    for c in sends:
        c.wait_send()
    for c in emits:
        c.wait()
    for d in range(1, C):
        remote(acts, xall.at[g], fs.at[d], xr.at[g], (mz, sib)).wait_send()
    for j in range(HL):
        for d in range(G - 1):
            remote(qs.at[j, 0], qr.at[j, 0], qas.at[j, d], qar.at[j, 0], (mz, sib)).wait_send()

    def sent(i, _):
        t, j = lax.div(i, HL), lax.rem(i, HL)

        @pl.when(t != mz)
        def _():
            remote(qpart.at[t, j], qrecv.at[j, mz], qzs.at[j, t], qzr.at[j, mz], (mz, sib)).wait_send()

        return 0

    lax.fori_loop(0, Z * HL, sent, 0)

    def scattered(i, _):
        k, n = lax.div(i, N), lax.rem(i, N)
        z, h = lax.div(n, G), lax.rem(n, G)

        @pl.when(n != me)
        def _():
            remote(cp.at[k, h], cr.at[k, mz, g], cas.at[k, z, h], car.at[k, mz, g],
                   (mz, sib)).wait_send()

        return 0

    lax.fori_loop(0, K * N, scattered, 0)


def body(activations, norm_gain, w_query, w_keyval, w_output, cache_keys, cache_values, lengths):
    Z = lax.axis_size("gx")
    G = lax.axis_size("gy")
    C = G // 2
    B, DL = activations.shape
    S, T, _ = cache_keys.shape
    QW = w_query.shape[1]
    HL = QW // HD
    BR = G * S
    K = S // SG
    NC = w_output.shape[1] // NCH
    V = pltpu.VMEM
    sem = pltpu.SemaphoreType.DMA
    scratch = [
        V((B, w_output.shape[1]), BF16), V((S, 2 * HD), BF16), pltpu.SMEM((S,), jnp.int32),
        V((DL,), F32), V((1, DL), F32),
        V(w_query.shape, BF16), V(w_keyval.shape, BF16), V(w_output.shape, BF16),
        V(cache_keys.shape, BF16), V(cache_values.shape, BF16),
        V((G, B, DL), BF16), V((G * B, DL), BF16),
        V((Z, B, 128), F32), V((G, B, 128), F32),
        V((Z, G, S, 2 * HD), F32), V((Z, S, 2 * HD), F32), V((S, HD), F32), V((S, HD), F32),
        V((Z, HL, BR, HD), F32), V((HL, Z, BR, HD), F32),
        V((HL, BR, HD), F32), V((HL, BR, HD), F32), V((2, S, HALF), F32),
        V((HL, G, S, HD), BF16), V((HL, G, S, HD), BF16),
        V((S, G * HL, HD), F32), V((S, G * HL, HD), F32),
        V((K, G, SG, QW), BF16), V((K, Z, G, SG, QW), BF16),
        V((K, Z * G * SG, QW), BF16),
        V((K, NCH, 2, C, C * SG, NC), F32), V((K, NCH, C, C * SG, NC), F32),
        V((K, NCH, C, C * SG, NC), BF16), V((K, NCH, C, C * SG, NC), BF16),
        sem((10,)), sem((C,)), sem((G,)), sem((C,)), sem((Z,)), sem((Z,)), sem((G,)), sem((G,)),
        sem((Z,)), sem((Z,)), sem((HL, Z)), sem((HL, Z)), sem((HL,)), sem((HL, G)), sem((HL, G)),
        sem((K, Z, G)), sem((K, Z, G)), sem((K, NCH)), sem((K, NCH)),
        sem((K, NCH, C)), sem((K, NCH, C)),
    ]
    anyspec = pl.BlockSpec(memory_space=pl.ANY)
    vspec = pl.BlockSpec(memory_space=pltpu.VMEM)
    shapes = (jax.ShapeDtypeStruct((B, w_output.shape[1]), BF16),
              jax.ShapeDtypeStruct((S, 2 * HD), BF16))
    attn, entries = pl.pallas_call(
        functools.partial(kernel, Z, G),
        out_shape=shapes,
        in_specs=[anyspec, anyspec, anyspec, anyspec, anyspec, anyspec, anyspec,
                  anyspec],
        out_specs=(anyspec, anyspec),
        scratch_shapes=scratch,
        compiler_params=pltpu.CompilerParams(
            collective_id=0, has_side_effects=True, vmem_limit_bytes=63 * 1024 * 1024),
        name="mqa_step",
    )(activations, norm_gain, w_query, w_keyval, w_output, cache_keys, cache_values,
      lengths)
    return pl.pallas_call(
        emit,
        out_shape=shapes,
        in_specs=[vspec, vspec],
        out_specs=(vspec, vspec),
        name="emit",
    )(attn, entries)


def solution(mesh):
    return jax.shard_map(
        body,
        mesh=mesh,
        in_specs=(
            P("gy", "gx"),
            P("gx"),
            P("gx", "gy"),
            P("gx", None),
            P("gy", "gx"),
            P(("gx", "gy"), None, None),
            P(("gx", "gy"), None, None),
            P(("gx", "gy")),
        ),
        out_specs=(P("gy", "gx"), P(("gx", "gy"), None)),
        check_vma=False,
    )
```

```python
import functools

import jax
import jax.numpy as jnp
from jax import lax
from jax.experimental import pallas as pl
from jax.experimental.pallas import tpu as pltpu
from jax.sharding import PartitionSpec as P

D = 18432
HD = 256
HALF = HD // 2
SG = 2
NCH = 3
LCH = 9
F32 = jnp.float32
BF16 = jnp.bfloat16
MESH = pl.DeviceIdType.MESH


def emit(a, b, c, d):
    c[...] = a[...]
    d[...] = b[...]


def kernel(Z, G, acts, gain_h, wq_h, wkv_h, wo_h, ck_h, cv_h, lens_h,
           out_h, new_h,
           out, new, lens, gain_1, gain, wq, wkv, wo, ck, cv, xall, normed, stz, stg, kvs, kvr, kro, vnew,
           qpart, qrecv, qrel, qsum, rot, qs, qr, qf, cf, cp, cr, ctx, ob, sb, os, orr,
           lsem, xs, xr, fs, zs, zr, gs, gr, kss, ksr, qzs, qzr, qrr, qas, qar,
           cas, car, bs, br, ohs, ohr):
    mz = lax.axis_index("gx")
    g = lax.axis_index("gy")
    C = G // 2
    chip = g // 2
    core = g % 2
    sib = g + 1 - 2 * core
    B, DL = acts.shape
    S = ck.shape[0]
    HL = wq.shape[1] // HD
    BR = G * S
    QW = wq.shape[1]
    K = S // SG
    NC = wo.shape[1] // NCH
    CW = DL // LCH
    sends = []

    zp = [lax.rem(mz + d, Z) for d in range(1, Z)]
    gp = [lax.rem(g + d, G) for d in range(1, G)]

    def peer(s):
        r, bit = 0, 1
        while bit < C:
            r = r + lax.rem(lax.div(chip, bit) + lax.div(s, bit), 2) * bit
            bit *= 2
        return r

    cpn = [peer(jnp.int32(d)) for d in range(1, C)]

    barrier = pltpu.get_barrier_semaphore()
    N = Z * G
    me = mz * G + g

    everyone = [(z, h) for z in zp for h in range(G)] + [(mz, h) for h in gp]
    for device in everyone:
        pl.semaphore_signal(barrier, inc=1, device_id=device, device_id_type=MESH)

    local = [pltpu.make_async_copy(a, b, lsem.at[i]) for i, (a, b) in enumerate(
        [(acts, xall.at[g]), (wkv_h, wkv), (wq_h, wq), (ck_h, ck), (cv_h, cv), (wo_h, wo)])]
    gcopy = pltpu.make_async_copy(gain_h, gain_1, lsem.at[6])
    lcopy = pltpu.make_async_copy(lens_h, lens, lsem.at[9])
    for i in (0, 2, 1, 3, 4, 5):
        local[i].start()
        if i == 0:
            gcopy.start()
            lcopy.start()
    line = Z == 4
    outer = (mz == 0) | (mz == Z - 1)
    low = mz < 2
    near = jnp.where(low, 1, 2)
    other = 3 - near
    edge = jnp.where(low, 0, 3)
    far = 3 - edge

    def remote(src, dst, ss, rs, dev):
        return pltpu.make_async_remote_copy(
            src_ref=src, dst_ref=dst, send_sem=ss, recv_sem=rs,
            device_id=dev, device_id_type=MESH)

    def push(src, dst, ss, rs, dev):
        c = remote(src, dst, ss, rs, dev)
        c.start()
        sends.append(c)

    def arrived(dst, rs):
        remote(dst, dst, rs, rs, (mz, sib)).wait_recv()

    local[0].wait()

    def stat(i, carry):
        a, b = carry
        x = xall[g, :, pl.ds(pl.multiple_of(i * CW, 128), CW)].astype(F32)
        return (a + jnp.sum(x, axis=1, keepdims=True),
                b + jnp.sum(x * x, axis=1, keepdims=True))

    zero = jnp.zeros((B, 1), F32)
    s1, s2 = lax.fori_loop(0, LCH, stat, (zero, zero))
    lane = lax.broadcasted_iota(jnp.int32, (B, 128), 1)
    stz[mz] = jnp.where(lane == 0, s1, s2)
    pl.semaphore_wait(barrier, N - 1)
    for d, z in enumerate(zp):
        push(stz.at[mz], stz.at[mz], zs.at[d], zr.at[mz], (z, g))

    def give(d):
        push(acts, xall.at[g], xs.at[d], xr.at[g], (mz, 2 * cpn[d - 1] + core))

    early = [d for d in range(1, C) if d & (d - 1) == 0]
    late = [d for d in range(1, C) if d & (d - 1)]
    for d in early:
        give(d)
    push(acts, xall.at[g], xs.at[0], xr.at[g], (mz, sib))

    lcopy.wait()
    index = lax.broadcasted_iota(jnp.int32, (1, HALF), 1)
    fine = jnp.ones((1, HALF), F32)
    coarse = jnp.ones((1, HALF), F32)
    for i in range(1, 16):
        fine = jnp.where(lax.rem(index, 16) == i, 10000.0 ** (-2.0 * i / HD), fine)
    for i in range(1, HALF // 16):
        coarse = jnp.where(lax.div(index, 16) == i, 10000.0 ** (-32.0 * i / HD), coarse)
    freq = fine * coarse
    angles = jnp.concatenate([freq * lens[s].astype(F32) for s in range(S)], axis=0)
    rot[0] = jnp.cos(angles)
    rot[1] = jnp.sin(angles)

    for z in zp:
        arrived(stz.at[z], zr.at[z])
    tot = stz[0]
    for z in range(1, Z):
        tot = tot + stz[z]
    stg[g] = tot
    for d, h in enumerate(gp):
        push(stg.at[g], stg.at[g], gs.at[d], gr.at[g], (mz, h))

    def normalize(c, i):
        t = jnp.concatenate([stg[2 * c], stg[2 * c + 1]], axis=0)
        mean = t[:, 0:1] / D
        var = t[:, 1:2] / D - mean * mean
        inv = lax.rsqrt(var + 1e-05)
        rows = pl.ds(pl.multiple_of(i * (2 * B), 16), 2 * B)

        def part(i, _):
            cols = pl.ds(pl.multiple_of(i * CW, 128), CW)
            x = jnp.concatenate([xall[2 * c, :, cols].astype(F32),
                                 xall[2 * c + 1, :, cols].astype(F32)], axis=0)
            normed[rows, cols] = ((x - mean) * inv * gain[:, cols]).astype(BF16)
            return 0

        lax.fori_loop(0, LCH, part, 0)

    def forward(s):
        b = 2 * peer(s) + core
        arrived(xall.at[b], xr.at[b])
        remote(xall.at[b], xall.at[b], fs.at[s], xr.at[b], (mz, sib)).start()

    def send_part(t, j):
        direct = jnp.logical_not((t == far) if line else (t == mz))

        @pl.when((t != mz) & direct)
        def _():
            remote(qpart.at[t, j], qrecv.at[j, mz], qzs.at[j, t], qzr.at[j, mz], (t, g)).start()

        if line:
            @pl.when((t == far) & outer)
            def _():
                remote(qpart.at[t, j], qrel.at[j], qzs.at[j, t], qrr.at[j], (near, g)).start()

    def relay(j):
        @pl.when(jnp.logical_not(outer))
        def _():
            arrived(qrel.at[j], qrr.at[j])
            qsum[j] = qpart[far, j] + qrel[j]
            remote(qsum.at[j], qrecv.at[j, mz], qzs.at[j, far], qzr.at[j, mz], (far, g)).start()

    own_step = 0
    bit = 1
    while bit < C:
        own_step = own_step + lax.rem(lax.div(chip, bit) + lax.div(mz, bit), 2) * bit
        bit *= 2

    def step(i):
        if line and C == Z:
            b0 = Z - 1 - mz
            b1 = b0 + 1 - 2 * lax.rem(b0, 2)
            b2 = mz + 1 - 2 * lax.rem(mz, 2)
            swap = b0 + chip == C - 1
            t0 = jnp.where(swap, b1, b0)
            t1 = jnp.where(swap, b0, b1)
            t = jnp.where(i == 0, t0, jnp.where(i == 1, t1, jnp.where(i == 2, b2, mz)))
            return peer(t)
        return jnp.where(i == C - 1, own_step, jnp.where(i < own_step, i, i + 1))

    gcopy.wait()
    gain[...] = gain_1[...].reshape(1, DL)
    arrived(xall.at[sib], xr.at[sib])
    arrived(stg.at[sib], gr.at[sib])

    for d in late:
        give(d)

    @pl.when(step(0) > 0)
    def _():
        forward(step(0))

    local[2].wait()

    def ready(i):
        s = step(i)
        t = peer(s)

        @pl.when(s > 0)
        def _():
            b = 2 * t + 1 - core
            arrived(xall.at[b], xr.at[b])
            arrived(stg.at[2 * t], gr.at[2 * t])
            arrived(stg.at[2 * t + 1], gr.at[2 * t + 1])

        normalize(t, i)
        return t

    def ahead(i):
        @pl.when(step(i) > 0)
        def _():
            forward(step(i))

    def stage(i, _):
        t = ready(i)
        rows = pl.ds(pl.multiple_of(i * (2 * B), 16), 2 * B)
        for j in range(HL):
            qpart[t, j] = jnp.dot(normed[rows, :], wq[:, j * HD:(j + 1) * HD],
                                  preferred_element_type=F32)
            send_part(t, j)
            if j == HL // 2:
                ahead(i + 1)
        return 0

    lax.fori_loop(0, C - 2, stage, 0)
    ahead(C - 1)
    t = ready(C - 2)
    ready(C - 1)
    for j in range(HL):
        part = jnp.dot(normed[(C - 2) * 2 * B:, :], wq[:, j * HD:(j + 1) * HD],
                       preferred_element_type=F32)
        qpart[t, j] = part[:2 * B]
        qpart[mz, j] = part[2 * B:]
        send_part(t, j)
        if line:
            relay(j)
    local[1].wait()
    part = jnp.dot(normed[...], wkv[...], preferred_element_type=F32)
    for i in range(C):
        z = peer(step(i))
        for h in range(G):
            r = i * BR + h * S
            kvs[z, h] = part[r:r + S]
    for d, z in enumerate(zp):
        push(kvs.at[z, g], kvr.at[mz], kss.at[d], ksr.at[mz], (z, g))

    co = rot[0]
    si = rot[1]

    def finish(j, _):
        if line:
            first = jnp.where(outer, near, edge)
            for z in (other, first):
                arrived(qrecv.at[j, z], qzr.at[j, z])

            @pl.when(jnp.logical_not(outer))
            def _():
                arrived(qrecv.at[j, far], qzr.at[j, far])
                qpart[mz, j] = qpart[mz, j] + qrecv[j, far]

            q = qpart[mz, j] + (qrecv[j, first] + qrecv[j, other])
        else:
            q = qpart[mz, j]
            for z in zp:
                arrived(qrecv.at[j, z], qzr.at[j, z])
                q = q + qrecv[j, z]
        for h in range(G):
            qs[j, h] = q[h * S:(h + 1) * S].astype(BF16)
        for d, h in enumerate(gp):
            remote(qs.at[j, h], qr.at[j, g], qas.at[j, d], qar.at[j, g], (mz, h)).start()
        qr[j, g] = qs[j, g]
        return 0

    lax.fori_loop(0, HL, finish, 0)
    for z in zp:
        arrived(kvr.at[z], ksr.at[z])
    kv = kvs[mz, g]
    for z in zp:
        kv = kv + kvr[z]
    kv = kv.astype(BF16)
    kf = kv.astype(F32)
    ka, kb = kf[:, :HALF], kf[:, HALF:HD]
    krot = jnp.concatenate([ka * co - kb * si, ka * si + kb * co], axis=1).astype(BF16)
    new[:, :HD] = krot
    new[:, HD:] = kv[:, HD:]
    kro[...] = krot.astype(F32)
    vnew[...] = kf[:, HD:]

    for j in range(HL):
        for h in gp:
            arrived(qr.at[j, h], qar.at[j, h])
        blocks = [qr[j, h].astype(F32) for h in range(G)]
        for s in range(S):
            rows = jnp.concatenate([b[s:s + 1] for b in blocks], axis=0)
            cs, sn = co[s:s + 1], si[s:s + 1]
            a = rows[:, :HALF]
            b = rows[:, HALF:]
            qf[s, j * G:(j + 1) * G, :] = jnp.concatenate(
                [a * cs - b * sn, a * sn + b * cs], axis=1)

    local[3].wait()
    local[4].wait()
    scale = 1.0 / HD**0.5

    def scores(s):
        qb = qf[s].astype(BF16)
        sc = lax.dot_general(qb, ck[s], (((1,), (1,)), ((), ())),
                             preferred_element_type=F32) * scale
        return qb, sc

    def weigh(s, qb, sc):
        valid = lax.broadcasted_iota(jnp.int32, sc.shape, 1) < lens[s]
        sc = jnp.where(valid, sc, -1e30)
        own = jnp.sum(qb.astype(F32) * kro[s:s + 1, :], axis=1, keepdims=True) * scale
        top = jnp.maximum(jnp.max(sc, axis=1, keepdims=True), own)
        p = jnp.where(valid, jnp.exp(sc - top), 0.0)
        po = jnp.exp(own - top)
        inv = 1.0 / (jnp.sum(p, axis=1, keepdims=True) + po)
        return (p * inv).astype(BF16), (po * inv).astype(BF16).astype(F32)

    def attend(group):
        first = [scores(s) for s in group]
        second = [weigh(s, *f) for s, f in zip(group, first)]
        for s, (w, wn) in zip(group, second):
            mixed = jnp.dot(w, cv[s], preferred_element_type=F32)
            mixed = mixed + wn * vnew[s:s + 1, :]
            cf[s] = mixed.astype(BF16).astype(F32)

    def scatter(k):
        for z, h in everyone:
            remote(cp.at[k, h], cr.at[k, mz, g], cas.at[k, z, h], car.at[k, mz, g], (z, h)).start()
        cr[k, mz, g] = cp[k, g]

    def gathered(k):
        for z, h in everyone:
            arrived(cr.at[k, z, h], car.at[k, z, h])
        for i in range(HL):
            cols = slice(i * HD, (i + 1) * HD)
            ctx[k, :, cols] = jnp.concatenate(
                [cr[k, z, h, :, cols].astype(F32) for z in range(Z) for h in range(G)],
                axis=0).astype(BF16)

    for k in range(K):
        attend(range(k * SG, (k + 1) * SG))
        for h in range(G):
            for i in range(HL):
                rows = jnp.concatenate(
                    [cf[s, i * G + h:i * G + h + 1, :] for s in range(k * SG, (k + 1) * SG)],
                    axis=0)
                cp[k, h, :, i * HD:(i + 1) * HD] = rows.astype(BF16)
        scatter(k)

    M = Z * G * SG
    PR = C * SG

    def cross(k, j):
        arrived(sb.at[k, j], br.at[k, j])
        for d, c2 in enumerate(cpn):
            os[k, j, c2] = (ob[k, j, core, c2] + sb[k, j, c2]).astype(BF16)
            push(os.at[k, j, c2], orr.at[k, j, chip], ohs.at[k, j, d], ohr.at[k, j, chip],
                 (mz, 2 * c2 + core))

    local[5].wait()
    pending = []
    for k in range(K):
        gathered(k)
        rows = ctx[k]
        for j in range(NCH):
            part = jnp.dot(rows, wo[:, j * NC:(j + 1) * NC], preferred_element_type=F32)
            for c in range(C):
                for p in range(2):
                    r = (2 * c + p) * PR
                    ob[k, j, p, c] = part[r:r + PR]
            push(ob.at[k, j, 1 - core], sb.at[k, j], bs.at[k, j], br.at[k, j], (mz, sib))
            for item in pending:
                cross(*item)
            pending = [(k, j)]
    for item in pending:
        cross(*item)
    src = lax.broadcasted_iota(jnp.int32, (B, B), 1)
    dst = lax.broadcasted_iota(jnp.int32, (B, B), 0)
    target = ((src % PR) // SG) * S + (src // PR) * SG + src % SG
    onehot = jnp.where(dst == target, 1.0, 0.0).astype(BF16)
    for j in range(NCH):
        groups = []
        for k in range(K):
            total = ob[k, j, core, chip] + sb[k, j, chip]
            for c2 in cpn:
                arrived(orr.at[k, j, c2], ohr.at[k, j, c2])
                total = total + orr[k, j, c2].astype(F32)
            groups.append(total)
        ordered = jnp.concatenate(groups, axis=0).astype(BF16)
        out[:, j * NC:(j + 1) * NC] = jnp.dot(
            onehot, ordered, preferred_element_type=F32).astype(BF16)
    emits = [pltpu.make_async_copy(out, out_h, lsem.at[7]),
             pltpu.make_async_copy(new, new_h, lsem.at[8])]
    for c in emits:
        c.start()
    for c in sends:
        c.wait_send()
    for c in emits:
        c.wait()
    for d in range(1, C):
        remote(acts, xall.at[g], fs.at[d], xr.at[g], (mz, sib)).wait_send()
    for j in range(HL):
        for d in range(G - 1):
            remote(qs.at[j, 0], qr.at[j, 0], qas.at[j, d], qar.at[j, 0], (mz, sib)).wait_send()

    def sent(i, _):
        t, j = lax.div(i, HL), lax.rem(i, HL)

        @pl.when(t != mz)
        def _():
            remote(qpart.at[t, j], qrecv.at[j, mz], qzs.at[j, t], qzr.at[j, mz], (mz, sib)).wait_send()

        return 0

    lax.fori_loop(0, Z * HL, sent, 0)

    def scattered(i, _):
        k, n = lax.div(i, N), lax.rem(i, N)
        z, h = lax.div(n, G), lax.rem(n, G)

        @pl.when(n != me)
        def _():
            remote(cp.at[k, h], cr.at[k, mz, g], cas.at[k, z, h], car.at[k, mz, g],
                   (mz, sib)).wait_send()

        return 0

    lax.fori_loop(0, K * N, scattered, 0)


def body(activations, norm_gain, w_query, w_keyval, w_output, cache_keys, cache_values, lengths):
    Z = lax.axis_size("gx")
    G = lax.axis_size("gy")
    C = G // 2
    B, DL = activations.shape
    S, T, _ = cache_keys.shape
    QW = w_query.shape[1]
    HL = QW // HD
    BR = G * S
    K = S // SG
    NC = w_output.shape[1] // NCH
    V = pltpu.VMEM
    sem = pltpu.SemaphoreType.DMA
    scratch = [
        V((B, w_output.shape[1]), BF16), V((S, 2 * HD), BF16), pltpu.SMEM((S,), jnp.int32),
        V((DL,), F32), V((1, DL), F32),
        V(w_query.shape, BF16), V(w_keyval.shape, BF16), V(w_output.shape, BF16),
        V(cache_keys.shape, BF16), V(cache_values.shape, BF16),
        V((G, B, DL), BF16), V((G * B, DL), BF16),
        V((Z, B, 128), F32), V((G, B, 128), F32),
        V((Z, G, S, 2 * HD), F32), V((Z, S, 2 * HD), F32), V((S, HD), F32), V((S, HD), F32),
        V((Z, HL, BR, HD), F32), V((HL, Z, BR, HD), F32),
        V((HL, BR, HD), F32), V((HL, BR, HD), F32), V((2, S, HALF), F32),
        V((HL, G, S, HD), BF16), V((HL, G, S, HD), BF16),
        V((S, G * HL, HD), F32), V((S, G * HL, HD), F32),
        V((K, G, SG, QW), BF16), V((K, Z, G, SG, QW), BF16),
        V((K, Z * G * SG, QW), BF16),
        V((K, NCH, 2, C, C * SG, NC), F32), V((K, NCH, C, C * SG, NC), F32),
        V((K, NCH, C, C * SG, NC), BF16), V((K, NCH, C, C * SG, NC), BF16),
        sem((10,)), sem((C,)), sem((G,)), sem((C,)), sem((Z,)), sem((Z,)), sem((G,)), sem((G,)),
        sem((Z,)), sem((Z,)), sem((HL, Z)), sem((HL, Z)), sem((HL,)), sem((HL, G)), sem((HL, G)),
        sem((K, Z, G)), sem((K, Z, G)), sem((K, NCH)), sem((K, NCH)),
        sem((K, NCH, C)), sem((K, NCH, C)),
    ]
    anyspec = pl.BlockSpec(memory_space=pl.ANY)
    vspec = pl.BlockSpec(memory_space=pltpu.VMEM)
    shapes = (jax.ShapeDtypeStruct((B, w_output.shape[1]), BF16),
              jax.ShapeDtypeStruct((S, 2 * HD), BF16))
    attn, entries = pl.pallas_call(
        functools.partial(kernel, Z, G),
        out_shape=shapes,
        in_specs=[anyspec, anyspec, anyspec, anyspec, anyspec, anyspec, anyspec,
                  anyspec],
        out_specs=(anyspec, anyspec),
        scratch_shapes=scratch,
        compiler_params=pltpu.CompilerParams(
            collective_id=0, has_side_effects=True, vmem_limit_bytes=63 * 1024 * 1024),
        name="mqa_step",
    )(activations, norm_gain, w_query, w_keyval, w_output, cache_keys, cache_values,
      lengths)
    return pl.pallas_call(
        emit,
        out_shape=shapes,
        in_specs=[vspec, vspec],
        out_specs=(vspec, vspec),
        name="emit",
    )(attn, entries)


def solution(mesh):
    return jax.shard_map(
        body,
        mesh=mesh,
        in_specs=(
            P("gy", "gx"),
            P("gx"),
            P("gx", "gy"),
            P("gx", None),
            P("gy", "gx"),
            P(("gx", "gy"), None, None),
            P(("gx", "gy"), None, None),
            P(("gx", "gy")),
        ),
        out_specs=(P("gy", "gx"), P(("gx", "gy"), None)),
        check_vma=False,
    )
```
